32 devices in a mesh: freq: 2 (over x), src: 16 (over z, y, core).
Axes of the slice: x: 2, y: 2, z: 4, core: 2. Of those that a mesh axis runs over, the one named last changes fastest.
Arguments:
- shots: bfloat16 [4, 8192, 8192], P('freq', 'src'), parts along dimension 0, may hold values from -6 to 6
- wavelet: float32 [4, 8192], P('freq', 'src'), parts along dimension 0, may hold values from -1.2 to 1.2
- obliquity: float32 [8192], P('src'), may hold values from 0.3 to 3
- aperture: int32 [64, 64, 4], P('src'), may hold values from -1 to 63, as said below
Outputs:
- multiples: bfloat16 [4, 8192, 8192], P('freq', None, 'src'), parts along dimension 0
The draws below stay inside these ranges and needn't reach their ends.
There are 2 independent parts, one for each index of `freq`. The reference program is written for one: setup_inputs(seed, part) draws one part's arguments, and reference() takes and returns one part's arrays. A program takes and returns all parts, laid end to end along the dimension named above; an argument that names none is the same for every part. Nothing has to cross between parts.
Inputs may be any that keep to these rules, and one draw needn't show every extreme that they name: `aperture`: entry (i, j, t) is -1 (unused) or a block k with |k - j| <= 2; no block stands twice in one list.
All inputs are finite; a program needn't handle non-finite values.
Results may differ from the reference program's by a relative error of at most 0.0072.
Values may be sent and summed in bfloat16 or wider, within the bound.
A program may use at most 192 MiB of HBM per device.

```python
import math
import jax
import jax.numpy as jnp
from jax import lax

N = 8192
BLK = 128
APW = 2
K_AP = 4
NB = 64


def draw_aperture(key, part):
    window_len = 2 * APW + 1
    scores = jax.random.randint(key, (NB, NB, window_len), 0, 1 << 20) * window_len + jnp.arange(window_len, dtype=jnp.int32)
    ordering = jnp.argsort(scores, axis=-1)[..., :K_AP].astype(jnp.int32)
    blocks = jnp.arange(NB, dtype=jnp.int32)[None, :, None] + ordering - APW
    dropped = jax.random.randint(jax.random.fold_in(key, 7), (NB, NB, K_AP), 0, 4)
    keeper = (blocks >= 0) & (blocks < NB) & ((dropped > 0) | (jnp.arange(K_AP)[None, None, :] == 0))
    return jnp.where(keeper, blocks, -1).astype(jnp.int32)


def level_of(key, dims, split, least, largest):
    def one(position, blocks):
        heights = jax.random.uniform(jax.random.fold_in(jax.random.fold_in(key, 6), position), (blocks,), jnp.float32, least / len(split), largest / len(split))
        return jnp.repeat(jnp.exp(heights), dims[position] // blocks).reshape((-1,) + (1,) * (len(dims) - position - 1))

    factor_of = one(*split[0])
    for cut in split[1:]:
        factor_of = factor_of * one(*cut)
    return factor_of


def scatter_about(own_key, shape, deviation, limit, cuts=(), held_as=jnp.bfloat16):
    result = jax.random.normal(own_key, shape, jnp.float32) * deviation
    if len(cuts) > 0:
        result = level_of(own_key, shape, cuts, -0.22, 0.18) * result
    return jnp.clip(result, min=-limit, max=limit).astype(held_as)


def setup_inputs(seed: int = 0, part: int = 0) -> dict:
    key_of = jax.random.split(jax.random.key(seed), 5)
    own_keys = jax.random.split(jax.random.fold_in(key_of[4], part), 5)
    return {
        "shots": scatter_about(own_keys[0], (2, N, N), 1.0, 6.0, ((1, 16),)),
        "wavelet": scatter_about(own_keys[1], (2, N), 0.2, 1.2, ((1, 16),), jnp.float32),
        "obliquity": jnp.clip(jnp.exp(math.log(3.0) - 2.3025851 * jax.random.uniform(key_of[2], (N,), jnp.float32) ** level_of(key_of[2], (N,), ((0, 16),), -0.2, 0.2)), 0.3, 3.0),
        "aperture": draw_aperture(jax.random.fold_in(key_of[4], 71), part),
    }


def complex_product(left_op, right_op):
    right_big = jnp.concatenate([jnp.concatenate([right_op[0], right_op[1]], axis=1), jnp.concatenate([-right_op[1], right_op[0]], axis=1)], axis=0)
    return -jnp.dot(left_op.astype(jnp.float32), right_big.astype(jnp.float32), preferred_element_type=jnp.float32, precision=lax.Precision.HIGHEST)


def reference(shots, wavelet, obliquity, aperture):
    shot_re = shots[0].astype(jnp.float32)
    shot_im = shots[1].astype(jnp.float32)
    wave_re = wavelet[0][:, None]
    wave_im = wavelet[1][:, None]
    scaled = jnp.stack([shot_re * wave_re - shot_im * wave_im, shot_re * wave_im + shot_im * wave_re]).astype(jnp.bfloat16)
    data = (scaled.astype(jnp.float32) * obliquity).astype(jnp.bfloat16)
    window_len = 2 * APW + 1
    rim_cols = APW * BLK
    colpad = jnp.pad(data, ((0, 0), (0, 0), (rim_cols, rim_cols)))
    rowpad = jnp.pad(data, ((0, 0), (rim_cols, rim_cols), (0, 0)))
    block_count = N // BLK

    def one_block(j):
        targets = j + jnp.arange(window_len, dtype=jnp.int32) - APW
        targets = jnp.where((targets >= 0) & (targets < block_count), targets, -2)
        lists = lax.dynamic_index_in_dim(aperture, j, 1, keepdims=False)
        block_mask = jnp.any(lists[:, :, None] == targets[None, None, :], axis=1)
        left_op = lax.dynamic_slice_in_dim(colpad, j * BLK, window_len * BLK, 2)
        left_op = left_op.reshape(2, block_count, BLK, window_len, BLK) * block_mask.astype(jnp.bfloat16)[None, :, None, :, None]
        left_op = jnp.concatenate([left_op[0].reshape(N, window_len * BLK), left_op[1].reshape(N, window_len * BLK)], axis=1)
        right_op = lax.dynamic_slice(rowpad, (jnp.int32(0), j * BLK, j * BLK), (2, window_len * BLK, BLK))
        return complex_product(left_op, right_op)

    results = lax.map(one_block, jnp.arange(block_count, dtype=jnp.int32))
    results = results.reshape(block_count, N, 2, BLK)
    results = jnp.transpose(results, (2, 1, 0, 3)).reshape(2, N, N)
    return results.astype(jnp.bfloat16)
```

```python
import functools

import jax
import jax.numpy as jnp
from jax import lax
from jax.experimental import pallas as pl
from jax.experimental.pallas import tpu as pltpu
from jax.sharding import PartitionSpec as P

BLK = 128
APW = 2
WIN = 2 * APW + 1
HALO = APW * BLK
SMALL_ROWS = 8


def xor_index(index, d):
    bit, result = 1, index
    while bit <= d:
        if d & bit:
            result = result + bit - 2 * bit * ((index // bit) % 2)
        bit *= 2
    return result


def exchange_kernel(n, rows, width, shots, small, recv, small_all,
                    base_s, base_r, mate_s, mate_r, ext_s, ext_r, sm_s, sm_r, loc):
    me = lax.axis_index("src")
    half = n // 2
    odd = me % 2
    mate = xor_index(me, 1)

    def edge(t):
        return (t == 0) | (t == n - 1)

    def middle(t):
        return (t == half - 1) | (t == half)

    def rows_of(s, col, wide):
        return recv.at[:, pl.ds(pl.multiple_of(s * rows, rows), rows), pl.ds(pl.multiple_of(col, BLK), wide)]

    def cols_of(col, wide):
        return shots.at[:, :, pl.ds(pl.multiple_of(col, BLK), wide)]

    def remote(src, dst, send, got, t):
        return pltpu.make_async_remote_copy(
            src_ref=src, dst_ref=dst, send_sem=send, recv_sem=got,
            device_id={"src": t}, device_id_type=pl.DeviceIdType.MESH)

    def span(t, wide_case, both):
        t_odd = t % 2
        if both:
            if wide_case:
                return t * width - HALO, 0, width + 2 * HALO
            return t * width - HALO * t_odd, HALO * (1 - t_odd), width + HALO
        if wide_case:
            return t * width - HALO * (1 - t_odd), HALO * t_odd, width + HALO
        return t * width, HALO, width

    def wide_for(t, d):
        if d < half:
            return jnp.logical_not(edge(t))
        return middle(t)

    def both_ways(cond, act):
        @pl.when(cond)
        def _():
            act(True)

        @pl.when(jnp.logical_not(cond))
        def _():
            act(False)

    def outgoing(d, wide_case):
        t = xor_index(me, d)
        src_col, dst_col, wide = span(t, wide_case, d <= 1)
        return remote(cols_of(src_col, wide), rows_of(me, dst_col, wide), base_s.at[d], base_r.at[d], t)

    def incoming(d, wide_case):
        s = xor_index(me, d)
        _, dst_col, wide = span(me, wide_case, d <= 1)
        place = rows_of(s, dst_col, wide)
        return remote(place, place, base_s.at[d], base_r.at[d], s)

    def own_copy(wide_case):
        src_col, dst_col, wide = span(me, wide_case, True)
        return pltpu.make_async_copy(cols_of(src_col, wide), rows_of(me, dst_col, wide), loc.at[0])

    def mate_out(d):
        s = xor_index(me, d)
        src = rows_of(s, width * (1 - odd) + HALO * odd, HALO)
        return remote(src, rows_of(s, (HALO + width) * odd, HALO), mate_s.at[d], mate_r.at[d], mate)

    def mate_in(d):
        place = rows_of(xor_index(mate, d), (HALO + width) * (1 - odd), HALO)
        return remote(place, place, mate_s.at[d], mate_r.at[d], mate)

    neighbour = me - 1 + 2 * odd
    hands_on = jnp.logical_not(edge(me) | middle(me))

    def ext_out(d):
        s = xor_index(me, d)
        src = rows_of(s, HALO * (1 - odd) + width * odd, HALO)
        return remote(src, rows_of(s, (HALO + width) * (1 - odd), HALO), ext_s.at[d], ext_r.at[d], neighbour)

    def ext_in(d):
        place = rows_of(xor_index(neighbour, d), (HALO + width) * odd, HALO)
        return remote(place, place, ext_s.at[d], ext_r.at[d], neighbour)

    def small_out(d):
        return remote(small, small_all.at[me], sm_s.at[d], sm_r.at[d], xor_index(me, d))

    def small_in(d):
        place = small_all.at[xor_index(me, d)]
        return remote(place, place, sm_s.at[d], sm_r.at[d], xor_index(me, d))

    barrier = pltpu.get_barrier_semaphore()
    for d in range(1, n):
        pl.semaphore_signal(barrier, inc=1, device_id={"src": xor_index(me, d)},
                            device_id_type=pl.DeviceIdType.MESH)
    pl.semaphore_wait(barrier, n - 1)

    far = list(range(n - 1, half - 1, -1))
    near = list(range(half - 1, 0, -1))
    order = [far[0]]
    for f, g in zip(far[1:], near):
        order += [g, f]

    for d in order:
        both_ways(wide_for(xor_index(me, d), d), lambda w, d=d: outgoing(d, w).start())
    both_ways(jnp.logical_not(edge(me)), lambda w: own_copy(w).start())
    small_own = pltpu.make_async_copy(small, small_all.at[me], loc.at[1])
    small_own.start()
    for d in range(1, n):
        small_out(d).start()

    for d in order:
        both_ways(wide_for(me, d), lambda w, d=d: incoming(d, w).wait_recv())
        if d > 1:
            mate_out(d).start()
        if d >= half:
            @pl.when(hands_on)
            def _(d=d):
                ext_out(d).start()

    for d in order:
        both_ways(wide_for(xor_index(me, d), d), lambda w, d=d: outgoing(d, w).wait_send())
        small_out(d).wait_send()
        small_in(d).wait_recv()
        if d > 1:
            mate_out(d).wait_send()
            mate_in(d).wait_recv()
        if d >= half:
            @pl.when(hands_on)
            def _(d=d):
                ext_out(d).wait_send()
                ext_in(d).wait_recv()
    both_ways(jnp.logical_not(edge(me)), lambda w: own_copy(w).wait())
    small_own.wait()


def product_kernel(rows, width, block_total, me_ref, aper, small, obl, recv, *rest):
    bands, out, rhs, left = rest[:-3], rest[-3], rest[-2], rest[-1]
    step = pl.program_id(0)
    me = me_ref[0]
    cols = width // BLK
    row_blocks = rows // BLK

    def make_data(block_ref, wave, start, wide):
        wave_re, wave_im = wave[:, 0:1], wave[:, 1:2]
        re = block_ref[0, :, start:start + wide].astype(jnp.float32)
        im = block_ref[1, :, start:start + wide].astype(jnp.float32)
        factor = obl[0:1, start:start + wide]
        s_re = (re * wave_re - im * wave_im).astype(jnp.bfloat16).astype(jnp.float32)
        s_im = (re * wave_im + im * wave_re).astype(jnp.bfloat16).astype(jnp.float32)
        return (s_re * factor).astype(jnp.bfloat16), (s_im * factor).astype(jnp.bfloat16)

    @pl.when(step == 0)
    def _():
        per = rows // HALO
        total = (block_total * BLK) // HALO
        for b, band in enumerate(bands):
            g = jnp.clip(me * (width // HALO) - 1 + b, 0, total - 1)
            lanes = pl.ds(pl.multiple_of((g % per) * HALO, BLK), HALO)
            wave = jnp.transpose(small[g // per, :, lanes])
            for j in range(cols):
                pair = [k for k in (APW * b, APW * b + 1) if 0 <= k - j < WIN]
                if not pair:
                    continue
                b_re, b_im = make_data(band, wave, HALO + j * BLK, BLK)
                for k in pair:
                    part = slice((k - APW * b) * BLK, (k - APW * b + 1) * BLK)
                    top = (k - j) * 2 * BLK
                    rhs[j, top:top + BLK, :BLK] = -b_re[part]
                    rhs[j, top:top + BLK, BLK:] = -b_im[part]
                    rhs[j, top + BLK:top + 2 * BLK, :BLK] = b_im[part]
                    rhs[j, top + BLK:top + 2 * BLK, BLK:] = -b_re[part]

    wave = jnp.transpose(small[step])
    for k in range(cols + 2 * APW):
        d_re, d_im = make_data(recv, wave, k * BLK, BLK)
        left[:, 2 * k * BLK:(2 * k + 1) * BLK] = d_re
        left[:, (2 * k + 1) * BLK:(2 * k + 2) * BLK] = d_im

    for j in range(cols):
        strips = []
        for r in range(row_blocks):
            listed = [aper[step * row_blocks + r, j * aper.shape[1] // cols + t] for t in range(aper.shape[1] // cols)]
            pieces = []
            for w in range(WIN):
                k = me * cols + j + w - APW
                hit = listed[0] == k
                for entry in listed[1:]:
                    hit = hit | (entry == k)
                hit = hit & (k >= 0) & (k < block_total)
                piece = left[r * BLK:(r + 1) * BLK, (j + w) * 2 * BLK:(j + w + 1) * 2 * BLK]
                pieces.append(jnp.where(hit, piece, jnp.zeros_like(piece)))
            strips.append(jnp.concatenate(pieces, axis=1))
        product = jnp.dot(jnp.concatenate(strips, axis=0), rhs[j], preferred_element_type=jnp.float32)
        out[0, :, j * BLK:(j + 1) * BLK] = product[:, :BLK].astype(jnp.bfloat16)
        out[1, :, j * BLK:(j + 1) * BLK] = product[:, BLK:].astype(jnp.bfloat16)


def per_device(n, shots, wavelet, obliquity, aperture):
    rows, total = shots.shape[1], shots.shape[2]
    width = total // n
    block_total = total // BLK
    row_blocks, _, entries = aperture.shape
    cols = width // BLK
    spread = width + 2 * HALO
    me = lax.axis_index("src")
    aper_rows = row_blocks * block_total * entries // rows
    small = jnp.concatenate([
        wavelet,
        obliquity[None, :],
        aperture.astype(jnp.float32).reshape(aper_rows, rows),
        jnp.zeros((SMALL_ROWS - 3 - aper_rows, rows), jnp.float32),
    ])
    anywhere = pl.BlockSpec(memory_space=pl.ANY)
    recv, small_all = pl.pallas_call(
        functools.partial(exchange_kernel, n, rows, width),
        out_shape=(
            jax.ShapeDtypeStruct((2, total, spread), shots.dtype),
            jax.ShapeDtypeStruct((n, SMALL_ROWS, rows), jnp.float32),
        ),
        in_specs=[anywhere, anywhere],
        out_specs=(anywhere, anywhere),
        scratch_shapes=[pltpu.SemaphoreType.DMA((n,))] * 8 + [pltpu.SemaphoreType.DMA((2,))],
        compiler_params=pltpu.CompilerParams(collective_id=0, has_side_effects=True),
    )(shots, small)

    aper = small_all[:, 3:3 + aper_rows].astype(jnp.int32).reshape(block_total, block_total * entries)
    aper = lax.dynamic_slice(aper, (jnp.int32(0), me * cols * entries), (block_total, cols * entries))
    before = lax.dynamic_slice(small_all, (jnp.maximum(me - 1, 0), 2, rows - HALO), (1, 1, HALO))
    after = lax.dynamic_slice(small_all, (jnp.minimum(me + 1, n - 1), 2, 0), (1, 1, HALO))
    obl = jnp.concatenate([before[0, 0], obliquity, after[0, 0]])[None, :]

    band_count = width // HALO + 2
    band_total = total // HALO


    return pl.pallas_call(
        functools.partial(product_kernel, rows, width, block_total),
        grid_spec=pltpu.PrefetchScalarGridSpec(
            num_scalar_prefetch=2,
            grid=(n,),
            in_specs=[
                pl.BlockSpec((n, SMALL_ROWS, rows), lambda i, *_: (0, 0, 0)),
                pl.BlockSpec((1, spread), lambda i, *_: (0, 0)),
                pl.BlockSpec((2, rows, spread), lambda i, *_: (0, i, 0)),
            ] + [
                pl.BlockSpec(
                    (2, HALO, spread),
                    lambda i, me_ref, aper_ref, b=b: (
                        0, jnp.clip(me_ref[0] * (width // HALO) - 1 + b, 0, band_total - 1), 0))
                for b in range(band_count)
            ],
            out_specs=pl.BlockSpec((2, rows, width), lambda i, *_: (0, i, 0)),
            scratch_shapes=[
                pltpu.VMEM((cols, WIN * 2 * BLK, 2 * BLK), jnp.bfloat16),
                pltpu.VMEM((rows, (cols + 2 * APW) * 2 * BLK), jnp.bfloat16),
            ],
        ),
        out_shape=jax.ShapeDtypeStruct((2, total, width), jnp.bfloat16),
        compiler_params=pltpu.CompilerParams(vmem_limit_bytes=48 * 1024 * 1024),
    )(me[None], aper, small_all, obl, recv, *([recv] * band_count))


def solution(mesh):
    return jax.shard_map(
        functools.partial(per_device, mesh.shape["src"]),
        mesh=mesh,
        in_specs=(P("freq", "src", None), P("freq", "src"), P("src"), P("src", None, None)),
        out_specs=P("freq", None, "src"),
        check_vma=False,
    )
```

```python
import functools

import jax
import jax.numpy as jnp
from jax import lax
from jax.experimental import pallas as pl
from jax.experimental.pallas import tpu as pltpu
from jax.sharding import PartitionSpec as P

BLK = 128
APW = 2
WIN = 2 * APW + 1
HALO = APW * BLK
SMALL_ROWS = 8
AHEAD = 3


def xor_index(index, d):
    bit, result = 1, index
    while bit <= d:
        if d & bit:
            result = result + bit - 2 * bit * ((index // bit) % 2)
        bit *= 2
    return result


def exchange_kernel(n, rows, width, shots, small, recv, small_all,
                    base_s, base_r, mate_s, mate_r, ext_s, ext_r, sm_s, sm_r, loc):
    me = lax.axis_index("src")
    half = n // 2
    odd = me % 2
    mate = xor_index(me, 1)

    def edge(t):
        return (t == 0) | (t == n - 1)

    def middle(t):
        return (t == half - 1) | (t == half)

    def rows_of(s, col, wide):
        return recv.at[:, pl.ds(pl.multiple_of(s * rows, rows), rows), pl.ds(pl.multiple_of(col, BLK), wide)]

    def cols_of(col, wide):
        return shots.at[:, :, pl.ds(pl.multiple_of(col, BLK), wide)]

    def remote(src, dst, send, got, t):
        return pltpu.make_async_remote_copy(
            src_ref=src, dst_ref=dst, send_sem=send, recv_sem=got,
            device_id={"src": t}, device_id_type=pl.DeviceIdType.MESH)

    def span(t, wide_case, both):
        t_odd = t % 2
        if both:
            if wide_case:
                return t * width - HALO, 0, width + 2 * HALO
            return t * width - HALO * t_odd, HALO * (1 - t_odd), width + HALO
        if wide_case:
            return t * width - HALO * (1 - t_odd), HALO * t_odd, width + HALO
        return t * width, HALO, width

    def wide_for(t, d):
        if d < half:
            return jnp.logical_not(edge(t))
        return middle(t)

    def both_ways(cond, act):
        @pl.when(cond)
        def _():
            act(True)

        @pl.when(jnp.logical_not(cond))
        def _():
            act(False)

    def outgoing(d, wide_case):
        t = xor_index(me, d)
        src_col, dst_col, wide = span(t, wide_case, d <= 1)
        return remote(cols_of(src_col, wide), rows_of(me, dst_col, wide), base_s.at[d], base_r.at[d], t)

    def incoming(d, wide_case):
        s = xor_index(me, d)
        _, dst_col, wide = span(me, wide_case, d <= 1)
        place = rows_of(s, dst_col, wide)
        return remote(place, place, base_s.at[d], base_r.at[d], s)

    def own_copy(wide_case):
        src_col, dst_col, wide = span(me, wide_case, True)
        return pltpu.make_async_copy(cols_of(src_col, wide), rows_of(me, dst_col, wide), loc.at[0])

    def mate_out(d):
        s = xor_index(me, d)
        src = rows_of(s, width * (1 - odd) + HALO * odd, HALO)
        return remote(src, rows_of(s, (HALO + width) * odd, HALO), mate_s.at[d], mate_r.at[d], mate)

    def mate_in(d):
        place = rows_of(xor_index(mate, d), (HALO + width) * (1 - odd), HALO)
        return remote(place, place, mate_s.at[d], mate_r.at[d], mate)

    neighbour = me - 1 + 2 * odd
    hands_on = jnp.logical_not(edge(me) | middle(me))

    def ext_out(d):
        s = xor_index(me, d)
        src = rows_of(s, HALO * (1 - odd) + width * odd, HALO)
        return remote(src, rows_of(s, (HALO + width) * (1 - odd), HALO), ext_s.at[d], ext_r.at[d], neighbour)

    def ext_in(d):
        place = rows_of(xor_index(neighbour, d), (HALO + width) * odd, HALO)
        return remote(place, place, ext_s.at[d], ext_r.at[d], neighbour)

    def small_out(d):
        return remote(small, small_all.at[me], sm_s.at[d], sm_r.at[d], xor_index(me, d))

    def small_in(d):
        place = small_all.at[xor_index(me, d)]
        return remote(place, place, sm_s.at[d], sm_r.at[d], xor_index(me, d))

    barrier = pltpu.get_barrier_semaphore()
    for d in range(1, n):
        pl.semaphore_signal(barrier, inc=1, device_id={"src": xor_index(me, d)},
                            device_id_type=pl.DeviceIdType.MESH)
    pl.semaphore_wait(barrier, n - 1)

    far = list(range(n - 1, half - 1, -1))
    near = list(range(half - 1, 0, -1))

    def sends(is_odd):
        return near + far if is_odd else far + near

    def arrivals(is_odd):
        place = {d: sends(bool(is_odd) != bool(d % 2)).index(d) for d in far + near}
        return sorted(far + near, key=lambda d: place[d])

    both_ways(jnp.logical_not(edge(me)), lambda w: own_copy(w).start())
    small_own = pltpu.make_async_copy(small, small_all.at[me], loc.at[1])
    small_own.start()
    for d in range(1, n):
        small_out(d).start()

    def run(is_odd):
        todo, come = sends(is_odd), arrivals(is_odd)
        for i in range(n - 1 + AHEAD):
            if i < n - 1:
                d = todo[i]
                both_ways(wide_for(xor_index(me, d), d), lambda w, d=d: outgoing(d, w).start())
            if i >= AHEAD:
                d = todo[i - AHEAD]
                both_ways(wide_for(xor_index(me, d), d), lambda w, d=d: outgoing(d, w).wait_send())
                d = come[i - AHEAD]
                both_ways(wide_for(me, d), lambda w, d=d: incoming(d, w).wait_recv())
                if d >= half:
                    @pl.when(hands_on)
                    def _(d=d):
                        ext_out(d).start()
                if d > 1:
                    mate_out(d).start()

    both_ways(odd == 1, run)

    for d in range(1, n):
        small_out(d).wait_send()
        small_in(d).wait_recv()
        if d > 1:
            mate_out(d).wait_send()
            mate_in(d).wait_recv()
        if d >= half:
            @pl.when(hands_on)
            def _(d=d):
                ext_out(d).wait_send()
                ext_in(d).wait_recv()
    both_ways(jnp.logical_not(edge(me)), lambda w: own_copy(w).wait())
    small_own.wait()


def product_kernel(rows, width, block_total, me_ref, aper, small, obl, recv, *rest):
    bands, out, rhs, left = rest[:-3], rest[-3], rest[-2], rest[-1]
    step = pl.program_id(0)
    me = me_ref[0]
    cols = width // BLK
    row_blocks = rows // BLK

    def make_data(block_ref, wave, start, wide):
        wave_re, wave_im = wave[:, 0:1], wave[:, 1:2]
        re = block_ref[0, :, start:start + wide].astype(jnp.float32)
        im = block_ref[1, :, start:start + wide].astype(jnp.float32)
        factor = obl[0:1, start:start + wide]
        s_re = (re * wave_re - im * wave_im).astype(jnp.bfloat16).astype(jnp.float32)
        s_im = (re * wave_im + im * wave_re).astype(jnp.bfloat16).astype(jnp.float32)
        return (s_re * factor).astype(jnp.bfloat16), (s_im * factor).astype(jnp.bfloat16)

    @pl.when(step == 0)
    def _():
        per = rows // HALO
        total = (block_total * BLK) // HALO
        for b, band in enumerate(bands):
            g = jnp.clip(me * (width // HALO) - 1 + b, 0, total - 1)
            lanes = pl.ds(pl.multiple_of((g % per) * HALO, BLK), HALO)
            wave = jnp.transpose(small[g // per, :, lanes])
            for j in range(cols):
                pair = [k for k in (APW * b, APW * b + 1) if 0 <= k - j < WIN]
                if not pair:
                    continue
                b_re, b_im = make_data(band, wave, HALO + j * BLK, BLK)
                for k in pair:
                    part = slice((k - APW * b) * BLK, (k - APW * b + 1) * BLK)
                    top = (k - j) * 2 * BLK
                    rhs[j, top:top + BLK, :BLK] = -b_re[part]
                    rhs[j, top:top + BLK, BLK:] = -b_im[part]
                    rhs[j, top + BLK:top + 2 * BLK, :BLK] = b_im[part]
                    rhs[j, top + BLK:top + 2 * BLK, BLK:] = -b_re[part]

    wave = jnp.transpose(small[step])
    for k in range(cols + 2 * APW):
        d_re, d_im = make_data(recv, wave, k * BLK, BLK)
        left[:, 2 * k * BLK:(2 * k + 1) * BLK] = d_re
        left[:, (2 * k + 1) * BLK:(2 * k + 2) * BLK] = d_im

    for j in range(cols):
        strips = []
        for r in range(row_blocks):
            listed = [aper[step * row_blocks + r, j * aper.shape[1] // cols + t] for t in range(aper.shape[1] // cols)]
            pieces = []
            for w in range(WIN):
                k = me * cols + j + w - APW
                hit = listed[0] == k
                for entry in listed[1:]:
                    hit = hit | (entry == k)
                hit = hit & (k >= 0) & (k < block_total)
                piece = left[r * BLK:(r + 1) * BLK, (j + w) * 2 * BLK:(j + w + 1) * 2 * BLK]
                pieces.append(jnp.where(hit, piece, jnp.zeros_like(piece)))
            strips.append(jnp.concatenate(pieces, axis=1))
        product = jnp.dot(jnp.concatenate(strips, axis=0), rhs[j], preferred_element_type=jnp.float32)
        out[0, :, j * BLK:(j + 1) * BLK] = product[:, :BLK].astype(jnp.bfloat16)
        out[1, :, j * BLK:(j + 1) * BLK] = product[:, BLK:].astype(jnp.bfloat16)


def per_device(n, shots, wavelet, obliquity, aperture):
    rows, total = shots.shape[1], shots.shape[2]
    width = total // n
    block_total = total // BLK
    row_blocks, _, entries = aperture.shape
    cols = width // BLK
    spread = width + 2 * HALO
    me = lax.axis_index("src")
    aper_rows = row_blocks * block_total * entries // rows
    small = jnp.concatenate([
        wavelet,
        obliquity[None, :],
        aperture.astype(jnp.float32).reshape(aper_rows, rows),
        jnp.zeros((SMALL_ROWS - 3 - aper_rows, rows), jnp.float32),
    ])
    anywhere = pl.BlockSpec(memory_space=pl.ANY)
    recv, small_all = pl.pallas_call(
        functools.partial(exchange_kernel, n, rows, width),
        out_shape=(
            jax.ShapeDtypeStruct((2, total, spread), shots.dtype),
            jax.ShapeDtypeStruct((n, SMALL_ROWS, rows), jnp.float32),
        ),
        in_specs=[anywhere, anywhere],
        out_specs=(anywhere, anywhere),
        scratch_shapes=[pltpu.SemaphoreType.DMA((n,))] * 8 + [pltpu.SemaphoreType.DMA((2,))],
        compiler_params=pltpu.CompilerParams(collective_id=0, has_side_effects=True),
    )(shots, small)

    aper = small_all[:, 3:3 + aper_rows].astype(jnp.int32).reshape(block_total, block_total * entries)
    aper = lax.dynamic_slice(aper, (jnp.int32(0), me * cols * entries), (block_total, cols * entries))
    before = lax.dynamic_slice(small_all, (jnp.maximum(me - 1, 0), 2, rows - HALO), (1, 1, HALO))
    after = lax.dynamic_slice(small_all, (jnp.minimum(me + 1, n - 1), 2, 0), (1, 1, HALO))
    obl = jnp.concatenate([before[0, 0], obliquity, after[0, 0]])[None, :]

    band_count = width // HALO + 2
    band_total = total // HALO


    return pl.pallas_call(
        functools.partial(product_kernel, rows, width, block_total),
        grid_spec=pltpu.PrefetchScalarGridSpec(
            num_scalar_prefetch=2,
            grid=(n,),
            in_specs=[
                pl.BlockSpec((n, SMALL_ROWS, rows), lambda i, *_: (0, 0, 0)),
                pl.BlockSpec((1, spread), lambda i, *_: (0, 0)),
                pl.BlockSpec((2, rows, spread), lambda i, *_: (0, i, 0)),
            ] + [
                pl.BlockSpec(
                    (2, HALO, spread),
                    lambda i, me_ref, aper_ref, b=b: (
                        0, jnp.clip(me_ref[0] * (width // HALO) - 1 + b, 0, band_total - 1), 0))
                for b in range(band_count)
            ],
            out_specs=pl.BlockSpec((2, rows, width), lambda i, *_: (0, i, 0)),
            scratch_shapes=[
                pltpu.VMEM((cols, WIN * 2 * BLK, 2 * BLK), jnp.bfloat16),
                pltpu.VMEM((rows, (cols + 2 * APW) * 2 * BLK), jnp.bfloat16),
            ],
        ),
        out_shape=jax.ShapeDtypeStruct((2, total, width), jnp.bfloat16),
        compiler_params=pltpu.CompilerParams(vmem_limit_bytes=48 * 1024 * 1024),
    )(me[None], aper, small_all, obl, recv, *([recv] * band_count))


def solution(mesh):
    return jax.shard_map(
        functools.partial(per_device, mesh.shape["src"]),
        mesh=mesh,
        in_specs=(P("freq", "src", None), P("freq", "src"), P("src"), P("src", None, None)),
        out_specs=P("freq", None, "src"),
        check_vma=False,
    )
```
